768 devices in a mesh: row: 32 (over y, z_hi, core), col: 24 (over x, z_lo).
Axes of the slice: x: 4, y: 8, z: 12 (z_hi: 2, z_lo: 6; z = z_hi * 6 + z_lo), core: 2. Of those that a mesh axis runs over, the one named last changes fastest.
Arguments:
- amplitudes: bfloat16 [6144, 6144], P('row', 'col'), may hold values from -6 to 6
- integrals: bfloat16 [6144, 6144], P('row', 'col'), may hold values from -0.078125 to 0.078125
- dressing: bfloat16 [6144, 3072], P(None, 'col'), may hold values from -0.078125 to 0.078125
Outputs:
- first_cycle: float32 [6144, 6144], P('row', 'col')
- second_cycle: float32 [6144, 3072], P('row', 'col')
The draws below stay inside these ranges and needn't reach their ends.
All inputs are finite; a program needn't handle non-finite values.
Results may differ from the reference program's by a relative error of at most 0.0029.
Values may be sent and summed in bfloat16 or wider, within the bound.
No kernel may reach another device: no remote copies, remote signals or barrier semaphores. Data moves between devices by JAX's collectives and lax.ppermute only.
A program may use at most 32 MiB of HBM per device.

```python
import jax
import jax.numpy as jnp

NV = 3072
OCC = 2
SLICE = 8
N_ROW = 32
N_COL = 24


def level_of(rng, shape, shards, smallest, high):
    level = 1.0
    for position, parts in shards:
        draws = jax.random.uniform(jax.random.fold_in(jax.random.fold_in(rng, 6), position), (parts,), jnp.float32, smallest / len(shards), high / len(shards))
        level = level * jnp.repeat(jnp.exp(draws), shape[position] // parts).reshape((-1,) + (1,) * (len(shape) - 1 - position))
    return level


def noise(stream_key, extent, spread, reach, split=(), dtype=jnp.bfloat16):
    gain = level_of(stream_key, extent, split, -0.22, 0.18) if split else 1.0
    values = jax.random.normal(stream_key, extent, jnp.float32) * spread * gain
    return jnp.minimum(jnp.maximum(values, -reach), reach).astype(dtype)


def setup_inputs(seed: int = 0) -> dict:
    splits = jax.random.split(jax.random.key(seed), 4)
    return {
        "amplitudes": noise(splits[0], (OCC * NV, OCC * NV), 1.0, 6.0, ((0, 32), (1, 24))),
        "integrals": noise(splits[1], (OCC * NV, OCC * NV), (OCC * NV) ** -0.5, 0.078125, ((0, 32), (1, 24))),
        "dressing": noise(splits[2], (OCC * NV, NV), (OCC * NV) ** -0.5, 0.078125, ((1, 24),)),
    }


def reference(amplitudes, integrals, dressing):
    first_cycle = jnp.dot(amplitudes, integrals, preferred_element_type=jnp.float32)
    rounded = first_cycle.astype(jnp.bfloat16)
    cycle = jnp.dot(rounded.T, dressing, preferred_element_type=jnp.float32)
    second_cycle = cycle.reshape(N_COL, N_ROW, SLICE, NV).transpose(1, 0, 2, 3).reshape(OCC * NV, NV)
    return first_cycle, second_cycle
```

```python
import jax
import jax.numpy as jnp
from jax import lax
from jax.experimental import pallas as pl
from jax.experimental.pallas import tpu as pltpu
from jax.sharding import Mesh, PartitionSpec as P


NY, NZH, NCO, NX, NZL = 8, 2, 2, 4, 6
ROW = ("y", "zh", "co")
COL = ("x", "zl")
OFFSETS = (0, -1, 1, -2, 2, -3, 3, 4)
F32, BF16 = jnp.float32, jnp.bfloat16
VMEM_SPEC = pl.BlockSpec(memory_space=pltpu.VMEM)


def shift(n, s):
    return [(i, (i + s) % n) for i in range(n)]


def first_kernel(a_ref, own_ref, other_ref, w_ref, wt_ref):
    y = lax.axis_index("y")
    upper = lax.axis_index("co") == 1
    total = jnp.zeros(w_ref.shape, F32)
    for step, offset in enumerate(OFFSETS):
        at = lax.rem(y + (offset + NY), NY) * 3
        rows = jnp.concatenate([a_ref[at], a_ref[at + 1], a_ref[at + 2]], axis=1)
        parts = []
        for zh in range(NZH):
            own, other = own_ref[step, zh], other_ref[step, zh]
            parts += [jnp.where(upper, other, own), jnp.where(upper, own, other)]
        total += jnp.dot(rows, jnp.concatenate(parts, axis=0), preferred_element_type=F32)
    w_ref[...] = total
    wt_ref[...] = total.T.reshape(wt_ref.shape).astype(BF16)


def second_kernel(w_ref, *refs):
    s_ref = refs[-1]
    x = lax.axis_index("x")
    for s in range(NX):
        s_ref[lax.rem(x + (NX - s), NX)] = jnp.dot(w_ref[...], refs[s][...], preferred_element_type=F32)


def permute(value, axis, n, s):
    return lax.ppermute(value, axis, shift(n, s))


def exchange(value, axis):
    return lax.all_to_all(value, axis, 0, 0, tiled=True)


def whole(amplitudes, integrals, dressing):
    rows, wide = amplitudes.shape
    deep = dressing.shape[0] // NX
    zh, x = lax.axis_index("zh"), lax.axis_index("x")

    a = exchange(jnp.broadcast_to(amplitudes[None], (NZL, rows, wide)), "zl")
    a = exchange(jnp.broadcast_to(a[None], (NX, NZL, rows, wide)), "x")
    a = a.reshape(NX * NZL, rows, wide)

    far = permute(integrals, "zh", NZH, 1)
    own = jnp.where(zh == 0, jnp.stack([integrals, far]), jnp.stack([far, integrals]))
    ahead = back = own
    held = [own]
    for _ in range(3):
        ahead = permute(ahead, "y", NY, 1)
        back = permute(back, "y", NY, -1)
        held += [ahead, back]
    last = jnp.stack([permute(ahead[0], "y", NY, 1), permute(back[1], "y", NY, -1)])
    held = jnp.stack(held + [last])
    other = permute(held, "co", NCO, 1)

    u = [lax.dynamic_slice_in_dim(dressing, x * deep, deep, 0)]
    for s in (1, 2, 3):
        piece = lax.dynamic_slice_in_dim(dressing, lax.rem(x + s, NX) * deep, deep, 0)
        u.append(permute(piece, "x", NX, s))

    first_cycle, wt = pl.pallas_call(
        first_kernel,
        out_shape=(
            jax.ShapeDtypeStruct((rows, wide), F32),
            jax.ShapeDtypeStruct((wide // 8, 8, rows), BF16),
        ),
        in_specs=[VMEM_SPEC] * 3,
        out_specs=(VMEM_SPEC,) * 2,
        name="first",
    )(a, held, other)

    wt = exchange(wt, ROW)
    wt = wt.reshape(NX, 8, 8, rows).transpose(0, 2, 1, 3).reshape(NX, 1, 8, deep)
    wt = jnp.broadcast_to(wt, (NX, NZL, 8, deep)).reshape(NX * NZL, 8, deep)
    wt = exchange(wt, COL).reshape(NX * NZL * 8, deep)

    part = pl.pallas_call(
        second_kernel,
        out_shape=jax.ShapeDtypeStruct((NX, NX * NZL * 8, dressing.shape[1]), F32),
        in_specs=[VMEM_SPEC] * 5,
        out_specs=VMEM_SPEC,
        name="second",
    )(wt, *u)
    part = exchange(part, "x")
    return first_cycle, jnp.sum(part, axis=0)


def solution(mesh):
    fine = Mesh(mesh.devices.reshape(NY, NZH, NCO, NX, NZL), ROW + COL)
    return jax.shard_map(
        whole,
        mesh=fine,
        in_specs=(P(ROW, COL), P(ROW, COL), P(None, COL)),
        out_specs=(P(ROW, COL), P(ROW, COL)),
        check_vma=False,
    )
```

```python
import jax
import jax.numpy as jnp
from jax import lax
from jax.experimental import pallas as pl
from jax.experimental.pallas import tpu as pltpu
from jax.sharding import Mesh, PartitionSpec as P


NY, NZH, NCO, NX, NZL = 8, 2, 2, 4, 6
ROW = ("y", "zh", "co")
COL = ("x", "zl")
F32, BF16 = jnp.float32, jnp.bfloat16
VMEM_SPEC = pl.BlockSpec(memory_space=pltpu.VMEM)


def shift(n, s):
    return [(i, (i + s) % n) for i in range(n)]


def permute(value, axis, n, s):
    return lax.ppermute(value, axis, shift(n, s))


def opposed(value, s):
    pairs = [
        (y * NCO + co, (y + (1 - 2 * co) * s) % NY * NCO + co) for y in range(NY) for co in range(NCO)
    ]
    return lax.ppermute(value, ("y", "co"), pairs)


def exchange(value, axis):
    return lax.all_to_all(value, axis, 0, 0, tiled=True)


def first_kernel(*refs):
    a_refs, v_refs, (w_ref, wt_ref, a_all, sems) = refs[:5], refs[5:14], refs[14:]
    x, y, co = lax.axis_index("x"), lax.axis_index("y"), lax.axis_index("co")
    way = 1 - 2 * co
    half = v_refs[4].shape[0]
    spots = [2 * x, 2 * lax.rem(x + 3, NX), 2 * lax.rem(x + 1, NX)]
    far = 2 * lax.rem(x + 2, NX)
    to = [a_all.at[pl.ds(s, 2)] for s in spots] + [a_all.at[far], a_all.at[far + 1]]
    copies = [pltpu.make_async_copy(r, t, sems.at[i]) for i, (r, t) in enumerate(zip(a_refs, to))]
    for copy in copies:
        copy.start()
    for copy in copies:
        copy.wait()

    def columns(step):
        at = lax.rem(y - way * step + NY, NY)
        return jnp.concatenate([a_all[at, j] for j in range(3)], axis=1)

    total = jnp.zeros(w_ref.shape, F32)
    for step, i in ((0, 0), (1, 1), (-1, 5), (2, 2), (-2, 6), (3, 3), (-3, 7)):
        total += jnp.dot(columns(step), v_refs[i][...], preferred_element_type=F32)
    a, mine, mates = columns(4), v_refs[4][...], v_refs[8][...]
    low, high = jnp.where(co == 0, mine, mates), jnp.where(co == 0, mates, mine)
    total += jnp.dot(a[:, :half], low, preferred_element_type=F32)
    total += jnp.dot(a[:, half:], high, preferred_element_type=F32)
    w_ref[...] = total
    wt_ref[...] = total.T.reshape(wt_ref.shape).astype(BF16)


def second_kernel(w_ref, *refs):
    s_ref = refs[-1]
    x = lax.axis_index("x")
    for s in range(NX):
        s_ref[lax.rem(x + (NX - s), NX)] = jnp.dot(w_ref[...], refs[s][...], preferred_element_type=F32)


def whole(amplitudes, integrals, dressing):
    rows, wide = amplitudes.shape
    deep = dressing.shape[0] // NX
    zh, co, x = lax.axis_index("zh"), lax.axis_index("co"), lax.axis_index("x")

    a = exchange(jnp.broadcast_to(amplitudes[None], (NZL, rows, wide)), "zl")
    a = a.reshape(2, 3, rows, wide)
    ahead, back = permute(a, "x", NX, 1), permute(a, "x", NX, -1)
    a = [a, ahead, back, permute(ahead[0], "x", NX, 1), permute(back[1], "x", NX, -1)]

    far = permute(integrals, "zh", NZH, 1)
    pair = jnp.where(zh == 0, jnp.stack([integrals, far]), jnp.stack([far, integrals]))
    mate = permute(pair, "co", NCO, 1)
    own = jnp.where(co == 0, jnp.stack([pair, mate], 1), jnp.stack([mate, pair], 1))
    own = own.reshape(NZH * NCO * rows, wide)
    one, two = opposed(own, 1), opposed(own, 2)
    three = opposed(two, 1)
    half = own.shape[0] // 2
    four = opposed(lax.dynamic_slice_in_dim(two, co * half, half, 0), 2)
    v = [own, one, two, three, four]
    v += [permute(v[i], "co", NCO, 1) for i in (1, 2, 3, 4)]

    u = [lax.dynamic_slice_in_dim(dressing, x * deep, deep, 0)]
    for s in (1, 2, 3):
        piece = lax.dynamic_slice_in_dim(dressing, lax.rem(x + s, NX) * deep, deep, 0)
        u.append(permute(piece, "x", NX, s))

    first_cycle, wt = pl.pallas_call(
        first_kernel,
        out_shape=(
            jax.ShapeDtypeStruct((rows, wide), F32),
            jax.ShapeDtypeStruct((wide // 8, 8, rows), BF16),
        ),
        in_specs=[VMEM_SPEC] * 14,
        out_specs=(VMEM_SPEC,) * 2,
        scratch_shapes=[pltpu.VMEM((2 * NX, 3, rows, wide), BF16), pltpu.SemaphoreType.DMA((5,))],
        compiler_params=pltpu.CompilerParams(vmem_limit_bytes=16 * 2**20),
        name="first",
    )(*a, *v)

    wt = exchange(wt, ROW)
    wt = wt.reshape(NX, 8, 8, rows).transpose(0, 2, 1, 3).reshape(NX, 1, 8, deep)
    wt = jnp.broadcast_to(wt, (NX, NZL, 8, deep)).reshape(NX * NZL, 8, deep)
    wt = exchange(wt, COL).reshape(NX * NZL * 8, deep)

    part = pl.pallas_call(
        second_kernel,
        out_shape=jax.ShapeDtypeStruct((NX, NX * NZL * 8, dressing.shape[1]), F32),
        in_specs=[VMEM_SPEC] * 5,
        out_specs=VMEM_SPEC,
        compiler_params=pltpu.CompilerParams(vmem_limit_bytes=16 * 2**20),
        name="second",
    )(wt, *u)
    part = exchange(part, "x")
    return first_cycle, jnp.sum(part, axis=0)


def solution(mesh):
    fine = Mesh(mesh.devices.reshape(NY, NZH, NCO, NX, NZL), ROW + COL)
    return jax.shard_map(
        whole,
        mesh=fine,
        in_specs=(P(ROW, COL), P(ROW, COL), P(None, COL)),
        out_specs=(P(ROW, COL), P(ROW, COL)),
        check_vma=False,
    )
```

```python
import jax
import jax.numpy as jnp
from jax import lax
from jax.experimental import pallas as pl
from jax.experimental.pallas import tpu as pltpu
from jax.sharding import Mesh, PartitionSpec as P


NY, NZH, NCO, NX, NZL = 8, 2, 2, 4, 6
ROW = ("y", "zh", "co")
COL = ("x", "zl")
F32, BF16 = jnp.float32, jnp.bfloat16
VMEM_SPEC = pl.BlockSpec(memory_space=pltpu.VMEM)


def shift(n, s):
    return [(i, (i + s) % n) for i in range(n)]


def permute(value, axis, n, s):
    return lax.ppermute(value, axis, shift(n, s))


def opposed(value, s):
    pairs = [
        (y * NCO + co, (y + (1 - 2 * co) * s) % NY * NCO + co) for y in range(NY) for co in range(NCO)
    ]
    return lax.ppermute(value, ("y", "co"), pairs)


def exchange(value, axis):
    return lax.all_to_all(value, axis, 0, 0, tiled=True)


def first_kernel(*refs):
    a_refs, v_refs, (w_ref, wt_ref, a_all, v_far, sems) = refs[:5], refs[5:14], refs[14:]
    x, y, co = lax.axis_index("x"), lax.axis_index("y"), lax.axis_index("co")
    spot = lax.rem(lax.axis_index("zl"), 3)
    way = 1 - 2 * co
    wide = w_ref.shape[1]
    half = v_refs[4].shape[0]
    spots = [2 * x, 2 * lax.rem(x + 3, NX), 2 * lax.rem(x + 1, NX)]
    far = 2 * lax.rem(x + 2, NX)
    to = [a_all.at[pl.ds(s, 2)] for s in spots] + [a_all.at[far], a_all.at[far + 1]]
    copies = [pltpu.make_async_copy(r, t, sems.at[i]) for i, (r, t) in enumerate(zip(a_refs, to))]
    for copy in copies:
        copy.start()
    v_far[pl.ds(pl.multiple_of(co * half, half), half)] = v_refs[4][...]
    v_far[pl.ds(pl.multiple_of((1 - co) * half, half), half)] = v_refs[8][...]
    for copy in copies:
        copy.wait()

    total = jnp.zeros(w_ref.shape, F32)
    v_all = {0: v_refs[0], 1: v_refs[1], -1: v_refs[5], 2: v_refs[2], -2: v_refs[6], 3: v_refs[3], -3: v_refs[7], 4: v_far}
    for step, v_ref in v_all.items():
        at = lax.rem(y - way * step + NY, NY)
        for j in range(3):
            start = pl.multiple_of(lax.rem(spot + 3 - j, 3) * wide, wide)
            total += jnp.dot(a_all[at, j], v_ref[pl.ds(start, wide)], preferred_element_type=F32)
    w_ref[...] = total
    wt_ref[...] = total.T.reshape(wt_ref.shape).astype(BF16)


def second_kernel(w_ref, *refs):
    s_ref = refs[-1]
    x = lax.axis_index("x")
    for s in range(NX):
        s_ref[lax.rem(x + (NX - s), NX)] = jnp.dot(w_ref[...], refs[s][...], preferred_element_type=F32)


def whole(amplitudes, integrals, dressing):
    rows, wide = amplitudes.shape
    deep = dressing.shape[0] // NX
    zh, co, x, zl = (lax.axis_index(n) for n in ("zh", "co", "x", "zl"))

    far = permute(amplitudes, "zl", NZL, 3)
    a = jnp.where(zl < 3, jnp.stack([amplitudes, far]), jnp.stack([far, amplitudes]))
    turns = [[(i, i // 3 * 3 + (i + s) % 3) for i in range(NZL)] for s in (1, 2)]
    a1 = lax.ppermute(a, "zl", turns[0])
    a2 = lax.ppermute(a, "zl", turns[1])
    a = jnp.stack([a, a1, a2], 1)
    ahead, back = permute(a, "x", NX, 1), permute(a, "x", NX, -1)
    a = [a, ahead, back, permute(ahead[0], "x", NX, 1), permute(back[1], "x", NX, -1)]

    far = permute(integrals, "zh", NZH, 1)
    pair = jnp.where(zh == 0, jnp.stack([integrals, far]), jnp.stack([far, integrals]))
    mate = permute(pair, "co", NCO, 1)
    own = jnp.where(co == 0, jnp.stack([pair, mate], 1), jnp.stack([mate, pair], 1))
    own = own.reshape(NZH * NCO * rows, wide)
    one, two = opposed(own, 1), opposed(own, 2)
    three = opposed(two, 1)
    half = own.shape[0] // 2
    four = opposed(lax.dynamic_slice_in_dim(two, co * half, half, 0), 2)
    v = [own, one, two, three, four]
    v += [permute(v[i], "co", NCO, 1) for i in (1, 2, 3, 4)]

    u = [lax.dynamic_slice_in_dim(dressing, x * deep, deep, 0)]
    for s in (1, 2, 3):
        piece = lax.dynamic_slice_in_dim(dressing, lax.rem(x + s, NX) * deep, deep, 0)
        u.append(permute(piece, "x", NX, s))

    first_cycle, wt = pl.pallas_call(
        first_kernel,
        out_shape=(
            jax.ShapeDtypeStruct((rows, wide), F32),
            jax.ShapeDtypeStruct((wide // 8, 8, rows), BF16),
        ),
        in_specs=[VMEM_SPEC] * 14,
        out_specs=(VMEM_SPEC,) * 2,
        scratch_shapes=[pltpu.VMEM((2 * NX, 3, rows, wide), BF16), pltpu.VMEM(own.shape, BF16), pltpu.SemaphoreType.DMA((5,))],
        compiler_params=pltpu.CompilerParams(vmem_limit_bytes=16 * 2**20),
        name="first",
    )(*a, *v)

    wt = exchange(wt, ROW)
    wt = wt.reshape(NX, 8, 8, rows).transpose(0, 2, 1, 3).reshape(NX, 1, 8, deep)
    wt = jnp.broadcast_to(wt, (NX, NZL, 8, deep)).reshape(NX * NZL, 8, deep)
    wt = exchange(wt, COL).reshape(NX * NZL * 8, deep)

    part = pl.pallas_call(
        second_kernel,
        out_shape=jax.ShapeDtypeStruct((NX, NX * NZL * 8, dressing.shape[1]), F32),
        in_specs=[VMEM_SPEC] * 5,
        out_specs=VMEM_SPEC,
        compiler_params=pltpu.CompilerParams(vmem_limit_bytes=16 * 2**20),
        name="second",
    )(wt, *u)
    part = exchange(part, "x")
    return first_cycle, jnp.sum(part, axis=0)


def solution(mesh):
    fine = Mesh(mesh.devices.reshape(NY, NZH, NCO, NX, NZL), ROW + COL)
    return jax.shard_map(
        whole,
        mesh=fine,
        in_specs=(P(ROW, COL), P(ROW, COL), P(None, COL)),
        out_specs=(P(ROW, COL), P(ROW, COL)),
        check_vma=False,
    )
```

```python
import jax
import jax.numpy as jnp
from jax import lax
from jax.experimental import pallas as pl
from jax.experimental.pallas import tpu as pltpu
from jax.sharding import Mesh, PartitionSpec as P


NY, NZH, NCO, NX, NZL = 8, 2, 2, 4, 6
ROW = ("y", "zh", "co")
COL = ("x", "zl")
F32, BF16 = jnp.float32, jnp.bfloat16
VMEM_SPEC = pl.BlockSpec(memory_space=pltpu.VMEM)


def shift(n, s):
    return [(i, (i + s) % n) for i in range(n)]


def permute(value, axis, n, s):
    return lax.ppermute(value, axis, shift(n, s))


def opposed(value, s):
    pairs = [
        (y * NCO + co, (y + (1 - 2 * co) * s) % NY * NCO + co) for y in range(NY) for co in range(NCO)
    ]
    return lax.ppermute(value, ("y", "co"), pairs)


def exchange(value, axis):
    return lax.all_to_all(value, axis, 0, 0, tiled=True)


def first_kernel(*refs):
    a_refs, v_refs, (w_ref, wt_ref, a_all, sems) = refs[:5], refs[5:14], refs[14:]
    x, y, co = lax.axis_index("x"), lax.axis_index("y"), lax.axis_index("co")
    way = 1 - 2 * co
    half = v_refs[4].shape[0]
    spots = [2 * x, 2 * lax.rem(x + 3, NX), 2 * lax.rem(x + 1, NX)]
    far = 2 * lax.rem(x + 2, NX)
    to = [a_all.at[pl.ds(s, 2)] for s in spots] + [a_all.at[far], a_all.at[far + 1]]
    copies = [pltpu.make_async_copy(r, t, sems.at[i]) for i, (r, t) in enumerate(zip(a_refs, to))]
    for copy in copies:
        copy.start()
    for copy in copies:
        copy.wait()

    def columns(step):
        at = lax.rem(y - way * step + NY, NY)
        return jnp.concatenate([a_all[at, j] for j in range(3)], axis=1)

    total = jnp.zeros(w_ref.shape, F32)
    for step, i in ((0, 0), (1, 1), (-1, 5), (2, 2), (-2, 6), (3, 3), (-3, 7)):
        total += jnp.dot(columns(step), v_refs[i][...], preferred_element_type=F32)
    a, mine, mates = columns(4), v_refs[4][...], v_refs[8][...]
    low, high = jnp.where(co == 0, mine, mates), jnp.where(co == 0, mates, mine)
    total += jnp.dot(a[:, :half], low, preferred_element_type=F32)
    total += jnp.dot(a[:, half:], high, preferred_element_type=F32)
    w_ref[...] = total
    turned = total.T.reshape((NY, NZH, NCO) + wt_ref.shape[3:])
    for zh in range(NZH):
        for c in range(NCO):
            wt_ref[:, c, zh] = turned[:, zh, c].astype(BF16)


def second_kernel(w_ref, *refs):
    s_ref = refs[-1]
    x = lax.axis_index("x")
    run = w_ref.shape[2] // 2
    for s in range(NX):
        total = jnp.zeros(s_ref.shape[1:], F32)
        for zh in range(NZH):
            for pair in range(2):
                rows = pl.ds((pair * NZH + zh) * run, run)
                total += jnp.dot(
                    w_ref[zh, :, pair * run : (pair + 1) * run], refs[s][rows], preferred_element_type=F32
                )
        s_ref[lax.rem(x + (NX - s), NX)] = total


def whole(amplitudes, integrals, dressing):
    rows, wide = amplitudes.shape
    deep = dressing.shape[0] // NX
    zh, co, x = lax.axis_index("zh"), lax.axis_index("co"), lax.axis_index("x")

    a = exchange(jnp.broadcast_to(amplitudes[None], (NZL, rows, wide)), "zl")
    a = a.reshape(2, 3, rows, wide)
    ahead, back = permute(a, "x", NX, 1), permute(a, "x", NX, -1)
    a = [a, ahead, back, permute(ahead[0], "x", NX, 1), permute(back[1], "x", NX, -1)]

    far = permute(integrals, "zh", NZH, 1)
    pair = jnp.where(zh == 0, jnp.stack([integrals, far]), jnp.stack([far, integrals]))
    mate = permute(pair, "co", NCO, 1)
    own = jnp.where(co == 0, jnp.stack([pair, mate], 1), jnp.stack([mate, pair], 1))
    own = own.reshape(NZH * NCO * rows, wide)
    one, two = opposed(own, 1), opposed(own, 2)
    three = opposed(two, 1)
    half = own.shape[0] // 2
    four = opposed(lax.dynamic_slice_in_dim(two, co * half, half, 0), 2)
    v = [own, one, two, three, four]
    v += [permute(v[i], "co", NCO, 1) for i in (1, 2, 3, 4)]

    u = [lax.dynamic_slice_in_dim(dressing, x * deep, deep, 0)]
    for s in (1, 2, 3):
        piece = lax.dynamic_slice_in_dim(dressing, lax.rem(x + s, NX) * deep, deep, 0)
        u.append(permute(piece, "x", NX, s))

    first_cycle, wt = pl.pallas_call(
        first_kernel,
        out_shape=(
            jax.ShapeDtypeStruct((rows, wide), F32),
            jax.ShapeDtypeStruct((NY, NCO, NZH, wide // (NY * NZH * NCO), rows), BF16),
        ),
        in_specs=[VMEM_SPEC] * 14,
        out_specs=(VMEM_SPEC,) * 2,
        scratch_shapes=[pltpu.VMEM((2 * NX, 3, rows, wide), BF16), pltpu.SemaphoreType.DMA((5,))],
        compiler_params=pltpu.CompilerParams(vmem_limit_bytes=16 * 2**20),
        name="first",
    )(*a, *v)

    deal = wt.shape[3]
    wt = exchange(wt.reshape(NY * NCO, NZH, deal, rows), ("y", "co"))
    wt = wt.reshape(NX, 4, NZH, deal, rows).transpose(2, 0, 3, 1, 4).reshape(NZH, NX, 1, deal, 4 * rows)
    wt = jnp.broadcast_to(wt, (NZH, NX, NZL, deal, 4 * rows)).reshape(NZH * NX * NZL, deal, 4 * rows)
    wt = exchange(wt, ("zh", "x", "zl")).reshape(NZH, NX * NZL * deal, 4 * rows)

    part = pl.pallas_call(
        second_kernel,
        out_shape=jax.ShapeDtypeStruct((NX, wt.shape[1], dressing.shape[1]), F32),
        in_specs=[VMEM_SPEC] * 5,
        out_specs=VMEM_SPEC,
        compiler_params=pltpu.CompilerParams(vmem_limit_bytes=16 * 2**20),
        name="second",
    )(wt, *u)
    part = exchange(part, "x")
    return first_cycle, jnp.sum(part, axis=0)


def solution(mesh):
    fine = Mesh(mesh.devices.reshape(NY, NZH, NCO, NX, NZL), ROW + COL)
    return jax.shard_map(
        whole,
        mesh=fine,
        in_specs=(P(ROW, COL), P(ROW, COL), P(None, COL)),
        out_specs=(P(ROW, COL), P(ROW, COL)),
        check_vma=False,
    )
```

```python
import jax
import jax.numpy as jnp
from jax import lax
from jax.experimental import pallas as pl
from jax.experimental.pallas import tpu as pltpu
from jax.sharding import Mesh, PartitionSpec as P


NY, NZH, NCO, NX, NZL = 8, 2, 2, 4, 6
ROW = ("y", "zh", "co")
COL = ("x", "zl")
F32, BF16 = jnp.float32, jnp.bfloat16
VMEM_SPEC = pl.BlockSpec(memory_space=pltpu.VMEM)


def shift(n, s):
    return [(i, (i + s) % n) for i in range(n)]


def permute(value, axis, n, s):
    return lax.ppermute(value, axis, shift(n, s))


def opposed(value, s):
    pairs = [
        (y * NCO + co, (y + (1 - 2 * co) * s) % NY * NCO + co) for y in range(NY) for co in range(NCO)
    ]
    return lax.ppermute(value, ("y", "co"), pairs)


def exchange(value, axis):
    return lax.all_to_all(value, axis, 0, 0, tiled=True)


def first_kernel(*refs):
    a_refs, v_refs, (w_ref, wt_ref, a_all, sems) = refs[:5], refs[5:14], refs[14:]
    x, y, co = lax.axis_index("x"), lax.axis_index("y"), lax.axis_index("co")
    way = 1 - 2 * co
    half = v_refs[4].shape[0]
    spots = [2 * x, 2 * lax.rem(x + 3, NX), 2 * lax.rem(x + 1, NX)]
    far = 2 * lax.rem(x + 2, NX)
    to = [a_all.at[pl.ds(s, 2)] for s in spots] + [a_all.at[far], a_all.at[far + 1]]
    copies = [pltpu.make_async_copy(r, t, sems.at[i]) for i, (r, t) in enumerate(zip(a_refs, to))]
    for copy in copies:
        copy.start()
    for copy in copies:
        copy.wait()

    def columns(step):
        at = lax.rem(y - way * step + NY, NY)
        return jnp.concatenate([a_all[at, j] for j in range(3)], axis=1)

    total = jnp.zeros(w_ref.shape, F32)
    for step, i in ((0, 0), (1, 1), (-1, 5), (2, 2), (-2, 6), (3, 3), (-3, 7)):
        total += jnp.dot(columns(step), v_refs[i][...], preferred_element_type=F32)
    a, mine, mates = columns(4), v_refs[4][...], v_refs[8][...]
    low, high = jnp.where(co == 0, mine, mates), jnp.where(co == 0, mates, mine)
    total += jnp.dot(a[:, :half], low, preferred_element_type=F32)
    total += jnp.dot(a[:, half:], high, preferred_element_type=F32)
    w_ref[...] = total
    turned = total.T.reshape((NY, NZH, NCO) + wt_ref.shape[3:])
    for zh in range(NZH):
        for c in range(NCO):
            wt_ref[:, c, zh] = turned[:, zh, c].astype(BF16)


def second_kernel(w_ref, *refs):
    s_ref = refs[-1]
    x = lax.axis_index("x")
    run = w_ref.shape[2] // 2
    for s in range(NX):
        total = jnp.zeros(s_ref.shape[1:], F32)
        for zh in range(NZH):
            for pair in range(2):
                rows = pl.ds((pair * NZH + zh) * run, run)
                total += jnp.dot(
                    w_ref[zh, :, pair * run : (pair + 1) * run], refs[s][rows], preferred_element_type=F32
                )
        s_ref[lax.rem(x + (NX - s), NX)] = total


def whole(amplitudes, integrals, dressing):
    rows, wide = amplitudes.shape
    deep = dressing.shape[0] // NX
    zh, co, x = lax.axis_index("zh"), lax.axis_index("co"), lax.axis_index("x")

    a = exchange(jnp.broadcast_to(amplitudes[None], (NZL, rows, wide)), "zl")
    a = a.reshape(2, 3, rows, wide)
    ahead, back = permute(a, "x", NX, 1), permute(a, "x", NX, -1)
    a = [a, ahead, back, permute(ahead[0], "x", NX, 1), permute(back[1], "x", NX, -1)]

    far = permute(integrals, "zh", NZH, 1)
    pair = jnp.where(zh == 0, jnp.stack([integrals, far]), jnp.stack([far, integrals]))
    mate = permute(pair, "co", NCO, 1)
    own = jnp.where(co == 0, jnp.stack([pair, mate], 1), jnp.stack([mate, pair], 1))
    own = own.reshape(NZH * NCO * rows, wide)
    one, two = opposed(own, 1), opposed(own, 2)
    three = opposed(two, 1)
    half = own.shape[0] // 2
    four = opposed(lax.dynamic_slice_in_dim(two, co * half, half, 0), 2)
    v = [own, one, two, three, four]
    v += [permute(v[i], "co", NCO, 1) for i in (1, 2, 3, 4)]

    u = [lax.dynamic_slice_in_dim(dressing, lax.rem(x + s, NX) * deep, deep, 0) for s in range(NX)]
    u = [u[0]] + [permute(u[s], "x", NX, s) for s in (1, 2, 3)]

    first_cycle, wt = pl.pallas_call(
        first_kernel,
        out_shape=(
            jax.ShapeDtypeStruct((rows, wide), F32),
            jax.ShapeDtypeStruct((NY, NCO, NZH, wide // (NY * NZH * NCO), rows), BF16),
        ),
        in_specs=[VMEM_SPEC] * 14,
        out_specs=(VMEM_SPEC,) * 2,
        scratch_shapes=[pltpu.VMEM((2 * NX, 3, rows, wide), BF16), pltpu.SemaphoreType.DMA((5,))],
        compiler_params=pltpu.CompilerParams(vmem_limit_bytes=16 * 2**20),
        name="first",
    )(*a, *v)

    deal = wt.shape[3]
    wt = exchange(wt.reshape(NY * NCO, NZH, deal, rows), ("y", "co"))
    wt = wt.reshape(NX, 4, NZH, deal, rows).transpose(2, 0, 3, 1, 4).reshape(NZH, NX, 1, deal, 4 * rows)
    wt = jnp.broadcast_to(wt, (NZH, NX, NZL, deal, 4 * rows)).reshape(NZH * NX * NZL, deal, 4 * rows)
    wt = exchange(wt, ("zh", "x", "zl")).reshape(NZH, NX * NZL * deal, 4 * rows)

    part = pl.pallas_call(
        second_kernel,
        out_shape=jax.ShapeDtypeStruct((NX, wt.shape[1], dressing.shape[1]), F32),
        in_specs=[VMEM_SPEC] * 5,
        out_specs=VMEM_SPEC,
        compiler_params=pltpu.CompilerParams(vmem_limit_bytes=16 * 2**20),
        name="second",
    )(wt, *u)
    part = exchange(part, "x")
    return first_cycle, jnp.sum(part, axis=0)


def solution(mesh):
    fine = Mesh(mesh.devices.reshape(NY, NZH, NCO, NX, NZL), ROW + COL)
    return jax.shard_map(
        whole,
        mesh=fine,
        in_specs=(P(ROW, COL), P(ROW, COL), P(None, COL)),
        out_specs=(P(ROW, COL), P(ROW, COL)),
        check_vma=False,
    )
```
